32 devices in a mesh: batch: 4 (over x, core), lat: 4 (over z), lon: 2 (over y).
Axes of the slice: x: 2, y: 2, z: 4, core: 2. Of those that a mesh axis runs over, the one named last changes fastest.
Arguments:
- tokens: bfloat16 [4, 2, 48, 48, 1024], P('batch', None, 'lat', 'lon'), may hold values from -6 to 6
- weights: bfloat16 [1024, 4096], P('batch')
- regions: int32 [2, 48, 48], P(None, 'lat', 'lon'), may hold values from 0 to 3
- offsets: int32 [2], replicated, may hold values from 1 to 11, as said below
Outputs:
- mixed: bfloat16 [4, 2, 48, 48, 1024], P('batch', None, 'lat', 'lon')
The draws below stay inside these ranges and needn't reach their ends.
Inputs may be any that keep to these rules, and one draw needn't show every extreme that they name: `offsets`: element 0 lies from 1 to 5; element 1 equals 11.
All inputs are finite; a program needn't handle non-finite values.
Results may differ from the reference program's by a relative error of at most 0.0042.
Values may be sent and summed in bfloat16 or wider, within the bound.
A program may use at most 128 MiB of HBM per device.

```python
import jax
import jax.numpy as jnp
from jax import lax

D = 1024
HEADS = 16
WLEV = 2
WLAT = 6
WLON = 12
LEV = 2
SAMPLES = 4
NLAT = 48
NLON = 48


def draw_weights(key, part):
    base = jax.random.normal(key, (D, 4 * D), jnp.float32) * D ** (-0.5)
    return base.astype(jnp.bfloat16)


def draw_offsets(key, part):
    first_key = jax.random.fold_in(key, 7)
    lat_shift = jax.random.randint(first_key, (1,), 1, WLAT)
    lon_shift = jnp.full((1,), WLON - 1, jnp.int32)
    return jnp.concatenate([lat_shift.astype(jnp.int32), lon_shift]).astype(jnp.int32)


def with_ends(entries, key, smallest, high):
    index_at = [jax.random.randint(jax.random.fold_in(key, axis), (), 0, length) for axis, length in enumerate(entries.shape)]
    longest = entries.shape.index(max(entries.shape))
    beside = index_at[:longest] + [(index_at[longest] + 1) % entries.shape[longest]] + index_at[longest + 1:]
    return entries.at[tuple(index_at)].set(smallest).at[tuple(beside)].set(high)


def block_levels(key, shape, pieces, least, high):
    factor_of = 1.0
    for position, parts in pieces:
        draws = jax.random.uniform(jax.random.fold_in(jax.random.fold_in(key, 6), position), (parts,), jnp.float32, least / len(pieces), high / len(pieces))
        factor_of = factor_of * jnp.repeat(jnp.exp(draws), shape[position] // parts).reshape((-1,) + (1,) * (len(shape) - 1 - position))
    return factor_of


def gaussian(key, shape, spread, most, shards=(), kind=jnp.bfloat16):
    result = spread * jax.random.normal(key, shape, jnp.float32)
    if shards:
        result = result * block_levels(key, shape, shards, -0.22, 0.18)
    return jnp.clip(result, -most, most).astype(kind)


def setup_inputs(seed: int = 0) -> dict:
    key_list = jax.random.split(jax.random.key(seed), 5)
    return {
        "tokens": gaussian(key_list[0], (SAMPLES, LEV, NLAT, NLON, D), 1.0, 6.0, ((0, 4), (2, 4), (3, 2))),
        "weights": draw_weights(jax.random.fold_in(key_list[4], 71), 0),
        "regions": with_ends(jax.random.randint(key_list[2], (LEV, NLAT, NLON), 0, 4), jax.random.fold_in(key_list[2], 1), 0, 3).astype(jnp.int32),
        "offsets": draw_offsets(jax.random.fold_in(key_list[4], 71), 0),
    }


def layer_norm(field):
    field = field.astype(jnp.float32)
    average = lax.optimization_barrier(jnp.mean(field, -1, keepdims=True))
    centred = field - average
    variance = lax.optimization_barrier(jnp.mean(centred * centred, -1, keepdims=True))
    return (centred * lax.rsqrt(variance + 1e-05)).astype(jnp.bfloat16)

def windows(field):
    levels, rows_lat, cols_lon, features = field.shape
    field = field.reshape(levels // WLEV, WLEV, rows_lat // WLAT, WLAT, cols_lon // WLON, WLON, features)
    field = field.transpose(0, 2, 4, 1, 3, 5, 6)
    return field.reshape(-1, WLEV * WLAT * WLON, features)

def unwindows(field, levels, rows_lat, cols_lon):
    features = field.shape[-1]
    field = field.reshape(levels // WLEV, rows_lat // WLAT, cols_lon // WLON, WLEV, WLAT, WLON, features)
    field = field.transpose(0, 3, 1, 4, 2, 5, 6)
    return field.reshape(levels, rows_lat, cols_lon, features)

def attend(normed, all_weights, regions):
    levels, rows_lat, cols_lon, width = normed.shape
    qkv = jnp.dot(normed.reshape(-1, width), all_weights[:, :3 * width], preferred_element_type=jnp.float32).astype(jnp.bfloat16)
    qkv = windows(qkv.reshape(levels, rows_lat, cols_lon, 3 * width))
    num_windows, win_size = (qkv.shape[0], qkv.shape[1])
    head_size = width // HEADS
    queries = qkv[..., :width].reshape(num_windows, win_size, HEADS, head_size).astype(jnp.float32)
    keys_all = qkv[..., width:2 * width].reshape(num_windows, win_size, HEADS, head_size).astype(jnp.float32)
    values_all = qkv[..., 2 * width:].reshape(num_windows, win_size, HEADS, head_size).astype(jnp.float32)
    scores = jnp.einsum('wqhe,wkhe->whqk', queries, keys_all) * head_size ** (-0.5)
    region_ids = windows(regions[..., None])[..., 0]
    allowed = region_ids[:, None, :, None] == region_ids[:, None, None, :]
    scores = jnp.where(allowed, scores, -1e+30)
    largest = lax.optimization_barrier(jnp.max(scores, -1, keepdims=True))
    expsc = jnp.exp(scores - largest)
    attn_probs = (expsc / lax.optimization_barrier(jnp.sum(expsc, -1, keepdims=True))).astype(jnp.bfloat16)
    mixed_out = jnp.einsum('whqk,wkhe->wqhe', attn_probs.astype(jnp.float32), values_all)
    mixed_out = mixed_out.astype(jnp.bfloat16).reshape(num_windows, win_size, width)
    return unwindows(mixed_out, levels, rows_lat, cols_lon)

def reference(tokens, weights, regions, offsets):

    def per_sample(sample):
        rolled = jnp.roll(sample, (-offsets[0], -offsets[1]), axis=(1, 2))
        attended = attend(layer_norm(rolled), weights, regions)
        back_rolled = jnp.roll(attended, (offsets[0], offsets[1]), axis=(1, 2))
        projected = jnp.dot(back_rolled.reshape(-1, D), weights[:, 3 * D:], preferred_element_type=jnp.float32)
        return (sample.astype(jnp.float32) + projected.reshape(sample.shape)).astype(jnp.bfloat16)
    return lax.map(per_sample, tokens)
```

```python
import functools

import jax
import jax.numpy as jnp
from jax import lax
from jax.experimental import pallas as pl
from jax.experimental.pallas import tpu as pltpu
from jax.sharding import PartitionSpec as P

HEADS = 16
WLEV = 2
WLAT = 6
WLON = 12
GROUPS = 4
HALO = WLAT - 1
OUTS = 4
CUTS = 2
MESH = pl.DeviceIdType.MESH


def normalise(x):
    average = jnp.mean(x, -1, keepdims=True)
    centred = x - average
    variance = jnp.mean(centred * centred, -1, keepdims=True)
    return centred * lax.rsqrt(variance + 1e-05)


def kernel(
    sizes,
    off_ref, tok_ref, w_ref, reg_ref, out_ref,
    wqkv, wout, own, ext, edge, near, diag, near_in, diag_in, edge_ext, reg_prev, ids, mask, xw, xn, qkv, ow, nat,
    ret, retn, retd, retn_in, retd_in, ret_ext, ymat,
    local_sem, w_send, w_recv, h_send, h_recv, r_send, r_recv, *attn,
):
    nb, nlat, nlon = sizes
    levels, rows, cols, width = tok_ref.shape
    win = WLEV * WLAT * WLON
    gw = width // GROUPS
    depth = w_ref.shape[0]
    half = depth // 2
    owid = width // OUTS
    chunks = GROUPS + OUTS
    chips = nb // 2
    nearp, diagp = edge_rows(rows)
    pad = nearp - rows
    b, lat, lon = lax.axis_index("batch"), lax.axis_index("lat"), lax.axis_index("lon")
    chip, core = b // 2, b % 2
    side = lon % 2

    def at(db=None, dlat=0, dlon=0):
        return (
            b if db is None else db,
            (lat + dlat + nlat) % nlat,
            (lon + dlon + nlon) % nlon,
        )

    partner = (chip * 2 + 1 - core, lat, lon)
    across = (b, lat, lon + 1 - 2 * side)
    far = [(((chip + k) % chips) * 2 + core, lat, lon) for k in range(1, chips)]
    greeted = [at(dlat=-1), at(dlat=1), at(dlat=-1, dlon=1), at(dlat=1, dlon=-1)] + far + [across, partner]
    if nlon > 2:
        greeted += [at(dlon=1), at(dlon=-1)]

    barrier = pltpu.get_barrier_semaphore()
    for device in greeted:
        pl.semaphore_signal(barrier, inc=1, device_id=device, device_id_type=MESH)

    def chunk(g):
        return wqkv.at[g] if g < GROUPS else wout.at[g - GROUPS]

    def own_loads(g):
        rows_here = pl.ds(pl.multiple_of(b * depth, depth), depth)
        if g >= GROUPS:
            return [pltpu.make_async_copy(
                w_ref.at[:, pl.ds(3 * width + (g - GROUPS) * owid, owid)],
                wout.at[g - GROUPS, rows_here],
                local_sem.at[2 * GROUPS + g])]
        return [
            pltpu.make_async_copy(
                w_ref.at[:, pl.ds(t * width + g * gw, gw)],
                wqkv.at[g, rows_here, pl.ds(t * gw, gw)],
                local_sem.at[3 * g + t],
            )
            for t in range(3)
        ]

    tok_load = pltpu.make_async_copy(tok_ref, own, local_sem.at[3 * GROUPS + OUTS])
    low_load = pltpu.make_async_copy(
        tok_ref.at[:, WLAT:rows], ext.at[:, 0:rows - WLAT], local_sem.at[3 * GROUPS + OUTS + 1])
    tok_load.start()
    loads = [own_loads(g) for g in range(chunks)]
    for group in loads:
        for c in group:
            c.start()
    low_load.start()

    def send(src, dst, ssem, rsem, device):
        c = pltpu.make_async_remote_copy(
            src_ref=src, dst_ref=dst, send_sem=ssem, recv_sem=rsem,
            device_id=device, device_id_type=MESH,
        )
        c.start()
        return c

    steps = [(g, i * (half // CUTS), half // CUTS) for g in range(GROUPS) for i in range(CUTS)]
    steps += [(GROUPS + n, 0, half) for n in range(OUTS)]

    def piece(p, owner, part):
        g, start, size = steps[p]
        return chunk(g).at[pl.ds(pl.multiple_of(owner * depth + part * half + start, size), size)]

    sent = []
    xs, ys = {}, {}
    core_copies = {g: [] for g in range(chunks)}

    def send_w(i, ref, device):
        c = send(ref, ref, w_send.at[i], w_recv.at[i], device)
        sent.append(c)
        return c

    def slot(p, k, j):
        return chunks + (p * (chips - 1) + k - 1) * 4 + j

    def first(g):
        for c in loads[g]:
            c.wait()
        mine = chunk(g).at[pl.ds(pl.multiple_of(b * depth, depth), depth)]
        core_copies[g].append(send_w(g, mine, partner))

    def cross(p):
        for k in range(1, chips):
            xs[p, k] = send_w(slot(p, k, 0), piece(p, b, side), far[k - 1])

    def origin(k):
        return ((chip + chips - k) % chips) * 2 + core

    def relay(p):
        if p >= len(steps):
            return
        for k in range(1, chips):
            xs[p, k].wait_recv()
            got = piece(p, origin(k), side)
            ys[p, k] = send_w(slot(p, k, 1), got, across)
            core_copies[steps[p][0]].append(send_w(slot(p, k, 2), got, partner))

    def finish(p):
        for k in range(1, chips):
            ys[p, k].wait_recv()
            core_copies[steps[p][0]].append(send_w(slot(p, k, 3), piece(p, origin(k), 1 - side), partner))

    def step(p):
        finish(p)
        relay(p + 2)

    def ready(g):
        for c in core_copies[g]:
            c.wait_recv()

    shift = off_ref[0]
    tok_load.wait()
    edge[...] = jnp.zeros_like(edge)
    for l in range(levels):
        for i in range(rows):
            row = own[l, i].astype(jnp.float32)[cols - 1:cols]
            edge[l * nearp + pad + i:l * nearp + pad + i + 1, :] = row
            if i < HALO:
                r = levels * nearp + l * diagp + i
                edge[r:r + 1, :] = row
    near[...] = edge[0:levels * nearp, :].astype(jnp.bfloat16)
    diag[...] = edge[levels * nearp:, :].astype(jnp.bfloat16)

    def masks(ref, k):
        for i in range(rows):
            ids[i * levels:(i + 1) * levels, :] = ref[i].astype(jnp.float32)
        table = ids[...].astype(jnp.bfloat16)
        pos = lax.broadcasted_iota(jnp.int32, (levels * rows, win), 1)
        which = lax.broadcasted_iota(jnp.int32, (levels * rows, win), 0)
        pos_t = lax.broadcasted_iota(jnp.int32, (win, levels * rows), 0)
        which_t = lax.broadcasted_iota(jnp.int32, (win, levels * rows), 1)
        col = (lax.broadcasted_iota(jnp.int32, (cols, win), 0)
               == k * WLON + lax.broadcasted_iota(jnp.int32, (cols, win), 1) % WLON)
        col_t = (lax.broadcasted_iota(jnp.int32, (win, cols), 1)
                 == k * WLON + lax.broadcasted_iota(jnp.int32, (win, cols), 0) % WLON)
        wide = jnp.dot(table, col.astype(jnp.float32).astype(jnp.bfloat16), preferred_element_type=jnp.float32)
        tall = lax.dot_general(
            col_t.astype(jnp.float32).astype(jnp.bfloat16), table, (((1,), (1,)), ((), ())),
            preferred_element_type=jnp.float32)

        def row_of(p, lw):
            return (lw * WLAT + p % (WLAT * WLON) // WLON) * levels + p // (WLAT * WLON)

        for lw in range(rows // WLAT):
            r = jnp.sum(jnp.where(which == row_of(pos, lw), wide, 0.0), 0, keepdims=True)
            c = jnp.sum(jnp.where(which_t == row_of(pos_t, lw), tall, 0.0), 1, keepdims=True)
            mask[lw * 2 + 1 - k] = (r == c).astype(jnp.float32)

    def norm(lw):
        src = own if lw == 0 else ext
        for l in range(levels):
            for ii in range(WLAT):
                x = normalise(src[l, ii + shift].astype(jnp.float32))
                base = lw * 2 * win + l * WLAT * WLON + ii * WLON
                xw[base + 1:base + WLON, :] = x[0:WLON - 1]
                xw[base + win:base + win + WLON, :] = x[WLON - 1:2 * WLON - 1]

    def norm_edges():
        x = normalise(near_in[...].astype(jnp.float32))
        e = normalise(diag_in[...].astype(jnp.float32))
        for l in range(levels):
            edge_ext[l, 0:nearp, :] = x[l * nearp:(l + 1) * nearp]
            edge_ext[l, nearp:nearp + diagp, :] = e[l * diagp:(l + 1) * diagp]

    def pack(lw):
        for l in range(levels):
            for ii in range(WLAT):
                base = lw * 2 * win + l * WLAT * WLON + ii * WLON
                xw[base:base + 1, :] = edge_ext[l, pl.ds(pad + lw * WLAT + ii + shift, 1), :]
        for w in range(2 * lw, 2 * lw + 2):
            xn[w * win:(w + 1) * win, :] = xw[w * win:(w + 1) * win, :].astype(jnp.bfloat16)

    norm(0)
    masks(reg_ref, 0)
    pl.semaphore_wait(barrier, len(greeted))

    for c in loads[0]:
        c.wait()
    loads[0] = []
    cross(0)
    lat_halo = send(tok_ref.at[:, 0:HALO], ext.at[:, rows - WLAT:rows - WLAT + HALO],
                    h_send.at[0], h_recv.at[0], at(dlat=-1))
    near_halo = send(near, near_in, h_send.at[2], h_recv.at[2], at(dlon=1))
    diag_halo = send(diag, diag_in, h_send.at[3], h_recv.at[3], at(dlat=-1, dlon=1))
    reg_halo = send(reg_ref, reg_prev, h_send.at[1], h_recv.at[1], at(dlon=1))
    halos = [lat_halo, reg_halo, near_halo, diag_halo]
    for g in range(chunks):
        first(g)
        for p in range(1, len(steps)):
            if steps[p][0] == g:
                cross(p)

    lane = lax.broadcasted_iota(jnp.int32, (win, 128), 1)
    ones = jnp.ones((win, 128), jnp.bfloat16)
    hs = width // HEADS

    def attention(g, lw):
        both = slice(lw * 2 * win, (lw + 1) * 2 * win)
        for t in range(3):
            part = jnp.dot(
                xn[both, :], wqkv[g, :, t * gw:(t + 1) * gw], preferred_element_type=jnp.float32
            ).astype(jnp.bfloat16)
            for w in range(2):
                qkv[w, :, t * gw:(t + 1) * gw] = part[w * win:(w + 1) * win]

        def window(w):
            allowed = mask[lw * 2 + w] > 0.5
            for pair in range(gw // 128):
                q = qkv[w, :, pair * 128:(pair + 1) * 128]
                k = qkv[w, :, gw + pair * 128:gw + (pair + 1) * 128]
                v = qkv[w, :, 2 * gw + pair * 128:2 * gw + (pair + 1) * 128]
                vones = jnp.concatenate([v, ones], axis=1)
                outs = []
                for h in range(128 // hs):
                    keep = (lane // hs == h).astype(jnp.float32) * (hs ** -0.5)
                    qh = (q.astype(jnp.float32) * keep).astype(jnp.bfloat16)
                    s = lax.dot_general(
                        qh, k, (((1,), (1,)), ((), ())), preferred_element_type=jnp.float32
                    )
                    s = jnp.where(allowed, s, -1e30)
                    e = jnp.exp(s - jnp.max(s, -1, keepdims=True)).astype(jnp.bfloat16)
                    o = jnp.dot(e, vones, preferred_element_type=jnp.float32)
                    outs.append(o[:, :128] / o[:, 128:])
                ow[w, :, pair * 128:(pair + 1) * 128] = jnp.where(lane < hs, outs[0], outs[1])

        for w in range(2):
            window(w)
        for l in range(levels):
            for ii in range(WLAT):
                i = lw * WLAT + ii
                r = l * WLAT * WLON + ii * WLON
                w = 0
                ret[l * nearp + i:l * nearp + i + 1, :] = ow[w, r:r + 1, :]
                if i >= rows - HALO:
                    d = levels * nearp + l * diagp + diagp - rows + i
                    ret[d:d + 1, :] = ow[w, r:r + 1, :]
                nat[l, i, 0:WLON - 1, :] = ow[w, r + 1:r + WLON, :]
                nat[l, i, WLON - 1:2 * WLON - 1, :] = ow[w + 1, r:r + WLON, :]
                attn[g][l, HALO + i] = nat[l, i].astype(jnp.bfloat16)

    def give_rows(g):
        return [
            send(attn[g].at[:, rows:rows + HALO], attn[g].at[:, 0:HALO],
                 r_send.at[3 * g], r_recv.at[3 * g], at(dlat=1)),
        ]

    def give_edges(g):
        retn[g] = ret[0:levels * nearp, :].astype(jnp.bfloat16)
        retd[g] = ret[levels * nearp:, :].astype(jnp.bfloat16)
        return [
            send(retn.at[g], retn_in.at[g], r_send.at[3 * g + 1], r_recv.at[3 * g + 1], at(dlon=-1)),
            send(retd.at[g], retd_in.at[g], r_send.at[3 * g + 2], r_recv.at[3 * g + 2], at(dlat=1, dlon=-1)),
        ]

    nat[:, :, cols - 1:cols, :] = jnp.zeros((levels, rows, 1, gw), jnp.float32)
    ret[...] = jnp.zeros_like(ret)
    row_id = lax.broadcasted_iota(jnp.int32, (cols, gw), 0)
    backs = []

    def gather(g):
        for c in backs[g]:
            c.wait_recv()
        n = retn_in[g].astype(jnp.float32)
        d = retd_in[g].astype(jnp.float32)
        for l in range(levels):
            ret_ext[l, 0:diagp, :] = d[l * diagp:(l + 1) * diagp]
            ret_ext[l, diagp:diagp + nearp, :] = n[l * nearp:(l + 1) * nearp]
        for l in range(levels):
            for i in range(rows):
                a = attn[g][l, HALO + i - shift].astype(jnp.float32)
                e = ret_ext[l, pl.ds(diagp + i - shift, 1), :]
                r = (l * rows + i) * cols
                ymat[r:r + cols, g * gw:(g + 1) * gw] = jnp.where(row_id == cols - 1, e, a)

    relay(0)
    near_halo.wait_recv()
    diag_halo.wait_recv()
    norm_edges()
    pack(0)
    relay(1)
    reg_halo.wait_recv()
    masks(reg_prev, 1)
    step(0)
    step(1)
    ready(0)
    attention(0, 0)
    step(2)
    low_load.wait()
    lat_halo.wait_recv()
    norm(1)
    pack(1)
    for g in range(GROUPS):
        if g > 0:
            ready(g)
        attention(g, 1)
        back = give_rows(g)
        if g == 0:
            step(3)
        else:
            step(2 * g + 2)
            attention(g, 0)
            step(2 * g + 3)
        backs.append(back + give_edges(g))
        if g > 0:
            gather(g - 1)
    for p in range(2 * GROUPS + 2, len(steps)):
        step(p)
    gather(GROUPS - 1)

    xn[...] = ymat[...].astype(jnp.bfloat16)
    for n in range(OUTS):
        ready(GROUPS + n)
        side_cols = slice(n * owid, (n + 1) * owid)
        p = jnp.dot(xn[...], wout[n], preferred_element_type=jnp.float32)
        for l in range(levels):
            t = own[l, :, :, side_cols].astype(jnp.float32)
            out_ref[l, :, :, side_cols] = (t + p[l * rows * cols:(l + 1) * rows * cols].reshape(t.shape)).astype(jnp.bfloat16)

    for c in sent + halos + sum(backs, []):
        c.wait_send()


def edge_rows(rows):
    return -(-rows // 16) * 16, 8


def local(sizes, tokens, weights, regions, offsets):
    block = tokens[0]
    levels, rows, cols, width = block.shape
    win = WLEV * WLAT * WLON
    nwin = (rows // WLAT) * (cols // WLON)
    gw = width // GROUPS
    nearp, diagp = edge_rows(rows)
    nw = GROUPS + OUTS + 4 * (GROUPS * CUTS + OUTS) * (sizes[0] // 2 - 1)
    bf, f32 = jnp.bfloat16, jnp.float32
    dma = pltpu.SemaphoreType.DMA
    anywhere = pl.BlockSpec(memory_space=pl.ANY)
    out = pl.pallas_call(
        functools.partial(kernel, sizes),
        out_shape=pltpu.VMEM(block.shape, bf),
        in_specs=[pl.BlockSpec(memory_space=pltpu.SMEM), anywhere, anywhere, pl.BlockSpec(memory_space=pltpu.VMEM)],
        out_specs=pl.BlockSpec(memory_space=pltpu.VMEM),
        scratch_shapes=[
            pltpu.VMEM((GROUPS, width, 3 * gw), bf),
            pltpu.VMEM((OUTS, width, width // OUTS), bf),
            pltpu.VMEM((levels, rows, cols, width), bf),
            pltpu.VMEM((levels, rows - WLAT + HALO, cols, width), bf),
            pltpu.VMEM((levels * (nearp + diagp), width), f32),
            pltpu.VMEM((levels * nearp, width), bf),
            pltpu.VMEM((levels * diagp, width), bf),
            pltpu.VMEM((levels * nearp, width), bf),
            pltpu.VMEM((levels * diagp, width), bf),
            pltpu.VMEM((levels, nearp + diagp, width), f32),
            pltpu.VMEM((rows, levels, cols), jnp.int32),
            pltpu.VMEM((levels * rows, cols), f32),
            pltpu.VMEM((nwin, win, win), f32),
            pltpu.VMEM((nwin * win, width), f32),
            pltpu.VMEM((nwin * win, width), bf),
            pltpu.VMEM((2, win, 3 * gw), bf),
            pltpu.VMEM((2, win, gw), f32),
            pltpu.VMEM((levels, rows, cols, gw), f32),
            pltpu.VMEM((levels * (nearp + diagp), gw), f32),
            pltpu.VMEM((GROUPS, levels * nearp, gw), bf),
            pltpu.VMEM((GROUPS, levels * diagp, gw), bf),
            pltpu.VMEM((GROUPS, levels * nearp, gw), bf),
            pltpu.VMEM((GROUPS, levels * diagp, gw), bf),
            pltpu.VMEM((levels, nearp + diagp, gw), f32),
            pltpu.VMEM((levels * rows * cols, width), f32),
            dma((3 * GROUPS + OUTS + 2,)),
            dma((nw,)),
            dma((nw,)),
            dma((4,)),
            dma((4,)),
            dma((3 * GROUPS,)),
            dma((3 * GROUPS,)),
        ]
        + [pltpu.VMEM((levels, rows + HALO, cols, gw), bf)] * GROUPS,
        compiler_params=pltpu.CompilerParams(
            collective_id=0, has_side_effects=True, vmem_limit_bytes=56 * 1024 * 1024
        ),
    )(offsets, block, weights, regions.transpose(1, 0, 2))
    return out[None]


def solution(mesh):
    sizes = (mesh.shape["batch"], mesh.shape["lat"], mesh.shape["lon"])
    in_specs = (P("batch", None, "lat", "lon", None), P("batch", None), P(None, "lat", "lon"), P())
    out_specs = P("batch", None, "lat", "lon", None)
    return jax.shard_map(
        functools.partial(local, sizes), mesh=mesh, in_specs=in_specs, out_specs=out_specs, check_vma=False
    )
```

```python
import functools

import jax
import jax.numpy as jnp
from jax import lax
from jax.experimental import pallas as pl
from jax.experimental.pallas import tpu as pltpu
from jax.sharding import PartitionSpec as P

HEADS = 16
WLEV = 2
WLAT = 6
WLON = 12
GROUPS = 4
HALO = WLAT - 1
OUTS = 4
CUTS = 2
MESH = pl.DeviceIdType.MESH


def plan(text):
    return tuple(tuple((e[0], int(e[1:])) for e in part.split()) for part in text.split(","))


PLAN = {
    "start": plan("r2 f0 r3 f1")[0],
    (0, 0): plan(",r4,f2"),
    (0, 1): plan(",r5,f3"),
    (1, 1): plan(",r6,f4"),
    (1, 0): plan(",r7,f5"),
    (2, 1): plan("r8,,r9 f6"),
    (2, 0): plan(",r10,f7 f8"),
    (3, 1): plan("r11,,f9"),
    (3, 0): plan(",f10,f11"),
}


def normalise(x):
    average = jnp.mean(x, -1, keepdims=True)
    centred = x - average
    variance = jnp.mean(centred * centred, -1, keepdims=True)
    return centred * lax.rsqrt(variance + 1e-05)


def kernel(
    sizes,
    off_ref, tok_ref, w_ref, reg_ref, out_ref,
    wqkv, wout, own, ext, edge, near, diag, near_in, diag_in, edge_ext, reg_prev, ids, mask, xw, xn, qkv, ow, nat,
    ret, retn, retd, retn_in, retd_in, ret_ext, ymat,
    local_sem, w_send, w_recv, h_send, h_recv, r_send, r_recv, ok_sem, *attn,
):
    nb, nlat, nlon = sizes
    levels, rows, cols, width = tok_ref.shape
    win = WLEV * WLAT * WLON
    gw = width // GROUPS
    depth = w_ref.shape[0]
    half = depth // 2
    owid = width // OUTS
    chunks = GROUPS + OUTS
    chips = nb // 2
    nearp, diagp = edge_rows(rows)
    pad = nearp - rows
    b, lat, lon = lax.axis_index("batch"), lax.axis_index("lat"), lax.axis_index("lon")
    chip, core = b // 2, b % 2
    side = lon % 2

    def at(db=None, dlat=0, dlon=0):
        return (
            b if db is None else db,
            (lat + dlat + nlat) % nlat,
            (lon + dlon + nlon) % nlon,
        )

    partner = (chip * 2 + 1 - core, lat, lon)
    across = (b, lat, lon + 1 - 2 * side)
    far = [(((chip + k) % chips) * 2 + core, lat, lon) for k in range(1, chips)]
    beside = [at(dlon=1), at(dlon=-1)] if nlon > 2 else []
    around = [at(dlat=-1), at(dlat=1), at(dlat=-1, dlon=1), at(dlat=1, dlon=-1)]

    barrier = pltpu.get_barrier_semaphore()

    def greet(devices, to):
        for _, z, y in devices:
            pl.semaphore_signal(barrier, inc=1, device_id=(to, z, y), device_id_type=MESH)

    @pl.when(core == 1)
    def _():
        pl.semaphore_signal(barrier, inc=1, device_id=partner, device_id_type=MESH)

    for device in far:
        greet([device], device[0] // 2 * 2)
    greet([across] + beside, chip * 2)
    greet(around, chip * 2 + 1)

    def meet_near():
        @pl.when(core == 0)
        def _():
            pl.semaphore_wait(barrier, 1 + 2 * (len(far) + 1 + len(beside)))
            pl.semaphore_signal(ok_sem.at[0], inc=1, device_id=partner, device_id_type=MESH)

        @pl.when(core == 1)
        def _():
            pl.semaphore_wait(ok_sem.at[0], 1)

    def meet_around():
        @pl.when(core == 1)
        def _():
            pl.semaphore_wait(barrier, 2 * len(around))
            pl.semaphore_signal(ok_sem.at[1], inc=1, device_id=partner, device_id_type=MESH)

        @pl.when(core == 0)
        def _():
            pl.semaphore_wait(ok_sem.at[1], 1)

    def chunk(g):
        return wqkv.at[g] if g < GROUPS else wout.at[g - GROUPS]

    def own_loads(g):
        rows_here = pl.ds(pl.multiple_of(b * depth, depth), depth)
        if g >= GROUPS:
            return [pltpu.make_async_copy(
                w_ref.at[:, pl.ds(3 * width + (g - GROUPS) * owid, owid)],
                wout.at[g - GROUPS, rows_here],
                local_sem.at[2 * GROUPS + g])]
        return [
            pltpu.make_async_copy(
                w_ref.at[:, pl.ds(t * width + g * gw, gw)],
                wqkv.at[g, rows_here, pl.ds(t * gw, gw)],
                local_sem.at[3 * g + t],
            )
            for t in range(3)
        ]

    tok_load = pltpu.make_async_copy(tok_ref, own, local_sem.at[3 * GROUPS + OUTS])
    low_load = pltpu.make_async_copy(
        tok_ref.at[:, WLAT:rows], ext.at[:, 0:rows - WLAT], local_sem.at[3 * GROUPS + OUTS + 1])
    tok_load.start()
    loads = [own_loads(g) for g in range(chunks)]
    for group in loads:
        for c in group:
            c.start()
    low_load.start()

    def send(src, dst, ssem, rsem, device):
        c = pltpu.make_async_remote_copy(
            src_ref=src, dst_ref=dst, send_sem=ssem, recv_sem=rsem,
            device_id=device, device_id_type=MESH,
        )
        c.start()
        return c

    steps = [(g, i * (half // CUTS), half // CUTS) for g in range(GROUPS) for i in range(CUTS)]
    steps += [(GROUPS + n, 0, half) for n in range(OUTS)]

    def piece(p, owner, part):
        g, start, size = steps[p]
        return chunk(g).at[pl.ds(pl.multiple_of(owner * depth + part * half + start, size), size)]

    sent = []
    xs, ys = {}, {}
    core_copies = {g: [] for g in range(chunks)}

    def send_w(i, ref, device):
        c = send(ref, ref, w_send.at[i], w_recv.at[i], device)
        sent.append(c)
        return c

    def slot(p, k, j):
        return chunks + (p * (chips - 1) + k - 1) * 4 + j

    def first(g):
        for c in loads[g]:
            c.wait()
        mine = chunk(g).at[pl.ds(pl.multiple_of(b * depth, depth), depth)]
        core_copies[g].append(send_w(g, mine, partner))

    def cross(p):
        for k in range(1, chips):
            xs[p, k] = send_w(slot(p, k, 0), piece(p, b, side), far[k - 1])

    def origin(k):
        return ((chip + chips - k) % chips) * 2 + core

    def relay(p):
        for k in range(1, chips):
            xs[p, k].wait_recv()
            got = piece(p, origin(k), side)
            ys[p, k] = send_w(slot(p, k, 1), got, across)
            core_copies[steps[p][0]].append(send_w(slot(p, k, 2), got, partner))

    def finish(p):
        for k in range(1, chips):
            ys[p, k].wait_recv()
            core_copies[steps[p][0]].append(send_w(slot(p, k, 3), piece(p, origin(k), 1 - side), partner))

    def pump(plan):
        for kind, p in plan:
            (relay if kind == "r" else finish)(p)

    def ready(g):
        for c in core_copies[g]:
            c.wait_recv()

    shift = off_ref[0]

    def masks(ref, k):
        for i in range(rows):
            ids[i * levels:(i + 1) * levels, :] = ref[i].astype(jnp.float32)
        table = ids[...].astype(jnp.bfloat16)
        pos = lax.broadcasted_iota(jnp.int32, (levels * rows, win), 1)
        which = lax.broadcasted_iota(jnp.int32, (levels * rows, win), 0)
        pos_t = lax.broadcasted_iota(jnp.int32, (win, levels * rows), 0)
        which_t = lax.broadcasted_iota(jnp.int32, (win, levels * rows), 1)
        col = (lax.broadcasted_iota(jnp.int32, (cols, win), 0)
               == k * WLON + lax.broadcasted_iota(jnp.int32, (cols, win), 1) % WLON)
        col_t = (lax.broadcasted_iota(jnp.int32, (win, cols), 1)
                 == k * WLON + lax.broadcasted_iota(jnp.int32, (win, cols), 0) % WLON)
        wide = jnp.dot(table, col.astype(jnp.float32).astype(jnp.bfloat16), preferred_element_type=jnp.float32)
        tall = lax.dot_general(
            col_t.astype(jnp.float32).astype(jnp.bfloat16), table, (((1,), (1,)), ((), ())),
            preferred_element_type=jnp.float32)

        def row_of(p, lw):
            return (lw * WLAT + p % (WLAT * WLON) // WLON) * levels + p // (WLAT * WLON)

        for lw in range(rows // WLAT):
            r = jnp.sum(jnp.where(which == row_of(pos, lw), wide, 0.0), 0, keepdims=True)
            c = jnp.sum(jnp.where(which_t == row_of(pos_t, lw), tall, 0.0), 1, keepdims=True)
            mask[lw * 2 + 1 - k] = (r == c).astype(jnp.float32)

    def norm(lw):
        src = own if lw == 0 else ext
        for l in range(levels):
            for ii in range(WLAT):
                x = normalise(src[l, ii + shift].astype(jnp.float32))
                base = lw * 2 * win + l * WLAT * WLON + ii * WLON
                xw[base + 1:base + WLON, :] = x[0:WLON - 1]
                xw[base + win:base + win + WLON, :] = x[WLON - 1:2 * WLON - 1]

    def norm_edges(ref, first_row, size):
        x = normalise(ref[...].astype(jnp.float32))
        for l in range(levels):
            edge_ext[l, first_row:first_row + size, :] = x[l * size:(l + 1) * size]

    def pack(lw):
        for l in range(levels):
            for ii in range(WLAT):
                base = lw * 2 * win + l * WLAT * WLON + ii * WLON
                xw[base:base + 1, :] = edge_ext[l, pl.ds(pad + lw * WLAT + ii + shift, 1), :]
        for w in range(2 * lw, 2 * lw + 2):
            xn[w * win:(w + 1) * win, :] = xw[w * win:(w + 1) * win, :].astype(jnp.bfloat16)

    def crosses(g):
        for c in loads[g]:
            c.wait()
        loads[g] = []
        for p in range(len(steps)):
            if steps[p][0] == g:
                cross(p)

    meet_near()
    crosses(0)
    first(0)
    reg_halo = send(reg_ref, reg_prev, h_send.at[1], h_recv.at[1], at(dlon=1))
    tok_load.wait()
    edge[...] = jnp.zeros_like(edge)
    for l in range(levels):
        for i in range(rows):
            row = own[l, i].astype(jnp.float32)[cols - 1:cols]
            edge[l * nearp + pad + i:l * nearp + pad + i + 1, :] = row
            if i < HALO:
                r = levels * nearp + l * diagp + i
                edge[r:r + 1, :] = row
    near[...] = edge[0:levels * nearp, :].astype(jnp.bfloat16)
    diag[...] = edge[levels * nearp:, :].astype(jnp.bfloat16)
    near_halo = send(near, near_in, h_send.at[2], h_recv.at[2], at(dlon=1))
    for g in range(1, chunks):
        crosses(g)
        first(g)
    norm(0)
    masks(reg_ref, 0)
    meet_around()
    diag_halo = send(diag, diag_in, h_send.at[3], h_recv.at[3], at(dlat=-1, dlon=1))
    lat_halo = send(tok_ref.at[:, 0:HALO], ext.at[:, rows - WLAT:rows - WLAT + HALO],
                    h_send.at[0], h_recv.at[0], at(dlat=-1))
    halos = [lat_halo, reg_halo, near_halo, diag_halo]

    lane = lax.broadcasted_iota(jnp.int32, (win, 128), 1)
    ones = jnp.ones((win, 128), jnp.bfloat16)
    hs = width // HEADS

    def attention(g, lw, after=((), (), ())):
        both = slice(lw * 2 * win, (lw + 1) * 2 * win)
        for t in range(3):
            part = jnp.dot(
                xn[both, :], wqkv[g, :, t * gw:(t + 1) * gw], preferred_element_type=jnp.float32
            ).astype(jnp.bfloat16)
            for w in range(2):
                qkv[w, :, t * gw:(t + 1) * gw] = part[w * win:(w + 1) * win]

        pump(after[0])

        def window(w):
            allowed = mask[lw * 2 + w] > 0.5
            for pair in range(gw // 128):
                q = qkv[w, :, pair * 128:(pair + 1) * 128]
                k = qkv[w, :, gw + pair * 128:gw + (pair + 1) * 128]
                v = qkv[w, :, 2 * gw + pair * 128:2 * gw + (pair + 1) * 128]
                vones = jnp.concatenate([v, ones], axis=1)
                outs = []
                for h in range(128 // hs):
                    keep = (lane // hs == h).astype(jnp.float32) * (hs ** -0.5)
                    qh = (q.astype(jnp.float32) * keep).astype(jnp.bfloat16)
                    s = lax.dot_general(
                        qh, k, (((1,), (1,)), ((), ())), preferred_element_type=jnp.float32
                    )
                    s = jnp.where(allowed, s, -1e30)
                    e = jnp.exp(s - jnp.max(s, -1, keepdims=True)).astype(jnp.bfloat16)
                    o = jnp.dot(e, vones, preferred_element_type=jnp.float32)
                    outs.append(o[:, :128] / o[:, 128:])
                ow[w, :, pair * 128:(pair + 1) * 128] = jnp.where(lane < hs, outs[0], outs[1])

        window(0)
        pump(after[1])
        window(1)
        pump(after[2])
        for l in range(levels):
            for ii in range(WLAT):
                i = lw * WLAT + ii
                r = l * WLAT * WLON + ii * WLON
                w = 0
                ret[l * nearp + i:l * nearp + i + 1, :] = ow[w, r:r + 1, :]
                if i >= rows - HALO:
                    d = levels * nearp + l * diagp + diagp - rows + i
                    ret[d:d + 1, :] = ow[w, r:r + 1, :]
                nat[l, i, 0:WLON - 1, :] = ow[w, r + 1:r + WLON, :]
                nat[l, i, WLON - 1:2 * WLON - 1, :] = ow[w + 1, r:r + WLON, :]
                attn[g][l, HALO + i] = nat[l, i].astype(jnp.bfloat16)

    def give_rows(g):
        return [
            send(attn[g].at[:, rows:rows + HALO], attn[g].at[:, 0:HALO],
                 r_send.at[3 * g], r_recv.at[3 * g], at(dlat=1)),
        ]

    def give_edges(g):
        retn[g] = ret[0:levels * nearp, :].astype(jnp.bfloat16)
        retd[g] = ret[levels * nearp:, :].astype(jnp.bfloat16)
        return [
            send(retn.at[g], retn_in.at[g], r_send.at[3 * g + 1], r_recv.at[3 * g + 1], at(dlon=-1)),
            send(retd.at[g], retd_in.at[g], r_send.at[3 * g + 2], r_recv.at[3 * g + 2], at(dlat=1, dlon=-1)),
        ]

    nat[:, :, cols - 1:cols, :] = jnp.zeros((levels, rows, 1, gw), jnp.float32)
    ret[...] = jnp.zeros_like(ret)
    row_id = lax.broadcasted_iota(jnp.int32, (cols, gw), 0)
    backs = []

    def gather(g):
        for c in backs[g]:
            c.wait_recv()
        n = retn_in[g].astype(jnp.float32)
        d = retd_in[g].astype(jnp.float32)
        for l in range(levels):
            ret_ext[l, 0:diagp, :] = d[l * diagp:(l + 1) * diagp]
            ret_ext[l, diagp:diagp + nearp, :] = n[l * nearp:(l + 1) * nearp]
        for l in range(levels):
            for i in range(rows):
                a = attn[g][l, HALO + i - shift].astype(jnp.float32)
                e = ret_ext[l, pl.ds(diagp + i - shift, 1), :]
                r = (l * rows + i) * cols
                ymat[r:r + cols, g * gw:(g + 1) * gw] = jnp.where(row_id == cols - 1, e, a)

    relay(0)
    near_halo.wait_recv()
    norm_edges(near_in, 0, nearp)
    pack(0)
    relay(1)
    reg_halo.wait_recv()
    masks(reg_prev, 1)
    pump(PLAN["start"])
    ready(0)
    attention(0, 0, PLAN[0, 0])
    low_load.wait()
    diag_halo.wait_recv()
    norm_edges(diag_in, nearp, diagp)
    lat_halo.wait_recv()
    norm(1)
    pack(1)
    for g in range(GROUPS):
        if g > 0:
            ready(g)
        attention(g, 1, PLAN[g, 1])
        back = give_rows(g)
        if g > 1:
            gather(g - 2)
        if g > 0:
            attention(g, 0, PLAN[g, 0])
        backs.append(back + give_edges(g))
    gather(GROUPS - 2)
    gather(GROUPS - 1)

    xn[...] = ymat[...].astype(jnp.bfloat16)
    for n in range(OUTS):
        ready(GROUPS + n)
        side_cols = slice(n * owid, (n + 1) * owid)
        p = jnp.dot(xn[...], wout[n], preferred_element_type=jnp.float32)
        for l in range(levels):
            t = own[l, :, :, side_cols].astype(jnp.float32)
            out_ref[l, :, :, side_cols] = (t + p[l * rows * cols:(l + 1) * rows * cols].reshape(t.shape)).astype(jnp.bfloat16)

    for c in sent + halos + sum(backs, []):
        c.wait_send()


def edge_rows(rows):
    return -(-rows // 16) * 16, 8


def local(sizes, tokens, weights, regions, offsets):
    block = tokens[0]
    levels, rows, cols, width = block.shape
    win = WLEV * WLAT * WLON
    nwin = (rows // WLAT) * (cols // WLON)
    gw = width // GROUPS
    nearp, diagp = edge_rows(rows)
    nw = GROUPS + OUTS + 4 * (GROUPS * CUTS + OUTS) * (sizes[0] // 2 - 1)
    bf, f32 = jnp.bfloat16, jnp.float32
    dma = pltpu.SemaphoreType.DMA
    anywhere = pl.BlockSpec(memory_space=pl.ANY)
    out = pl.pallas_call(
        functools.partial(kernel, sizes),
        out_shape=pltpu.VMEM(block.shape, bf),
        in_specs=[pl.BlockSpec(memory_space=pltpu.SMEM), anywhere, anywhere, pl.BlockSpec(memory_space=pltpu.VMEM)],
        out_specs=pl.BlockSpec(memory_space=pltpu.VMEM),
        scratch_shapes=[
            pltpu.VMEM((GROUPS, width, 3 * gw), bf),
            pltpu.VMEM((OUTS, width, width // OUTS), bf),
            pltpu.VMEM((levels, rows, cols, width), bf),
            pltpu.VMEM((levels, rows - WLAT + HALO, cols, width), bf),
            pltpu.VMEM((levels * (nearp + diagp), width), f32),
            pltpu.VMEM((levels * nearp, width), bf),
            pltpu.VMEM((levels * diagp, width), bf),
            pltpu.VMEM((levels * nearp, width), bf),
            pltpu.VMEM((levels * diagp, width), bf),
            pltpu.VMEM((levels, nearp + diagp, width), f32),
            pltpu.VMEM((rows, levels, cols), jnp.int32),
            pltpu.VMEM((levels * rows, cols), f32),
            pltpu.VMEM((nwin, win, win), f32),
            pltpu.VMEM((nwin * win, width), f32),
            pltpu.VMEM((nwin * win, width), bf),
            pltpu.VMEM((2, win, 3 * gw), bf),
            pltpu.VMEM((2, win, gw), f32),
            pltpu.VMEM((levels, rows, cols, gw), f32),
            pltpu.VMEM((levels * (nearp + diagp), gw), f32),
            pltpu.VMEM((GROUPS, levels * nearp, gw), bf),
            pltpu.VMEM((GROUPS, levels * diagp, gw), bf),
            pltpu.VMEM((GROUPS, levels * nearp, gw), bf),
            pltpu.VMEM((GROUPS, levels * diagp, gw), bf),
            pltpu.VMEM((levels, nearp + diagp, gw), f32),
            pltpu.VMEM((levels * rows * cols, width), f32),
            dma((3 * GROUPS + OUTS + 2,)),
            dma((nw,)),
            dma((nw,)),
            dma((4,)),
            dma((4,)),
            dma((3 * GROUPS,)),
            dma((3 * GROUPS,)),
        ]
        + [pltpu.SemaphoreType.REGULAR((2,))]
        + [pltpu.VMEM((levels, rows + HALO, cols, gw), bf)] * GROUPS,
        compiler_params=pltpu.CompilerParams(
            collective_id=0, has_side_effects=True, vmem_limit_bytes=56 * 1024 * 1024
        ),
    )(offsets, block, weights, regions.transpose(1, 0, 2))
    return out[None]


def solution(mesh):
    sizes = (mesh.shape["batch"], mesh.shape["lat"], mesh.shape["lon"])
    in_specs = (P("batch", None, "lat", "lon", None), P("batch", None), P(None, "lat", "lon"), P())
    out_specs = P("batch", None, "lat", "lon", None)
    return jax.shard_map(
        functools.partial(local, sizes), mesh=mesh, in_specs=in_specs, out_specs=out_specs, check_vma=False
    )
```

```python
import functools

import jax
import jax.numpy as jnp
from jax import lax
from jax.experimental import pallas as pl
from jax.experimental.pallas import tpu as pltpu
from jax.sharding import PartitionSpec as P

HEADS = 16
WLEV = 2
WLAT = 6
WLON = 12
GROUPS = 4
HALO = WLAT - 1
OUTS = 4
CUTS = 2
DIRECT = 2
MESH = pl.DeviceIdType.MESH


def plan(text):
    return tuple(tuple((e[0], int(e[1:])) for e in part.split()) for part in text.split(","))


PLAN = {
    "start": plan("r2 f0 r3 f1")[0],
    (0, 0): plan(",r4,f2 r5"),
    (0, 1): plan("f3,,"),
    (1, 1): plan("r6,f4,"),
    (1, 0): plan("r7,f5,"),
    (2, 1): plan("r8 f6,r9,f7 r10"),
    (3, 1): plan(",f8,r11"),
    (2, 0): plan("f9,,"),
    (3, 0): plan(",,"),
}


def normalise(x):
    average = jnp.mean(x, -1, keepdims=True)
    centred = x - average
    variance = jnp.mean(centred * centred, -1, keepdims=True)
    return centred * lax.rsqrt(variance + 1e-05)


def kernel(
    sizes,
    off_ref, tok_ref, w_ref, reg_ref, out_ref,
    wqkv, wout, own, ext, edge, near, diag, near_in, diag_in, edge_ext, reg_prev, ids, mask, mask_rest, keep, xw, xn, qkv, ow, nat,
    ret, retn, retd, retn_in, retd_in, ret_ext, ymat, acc,
    local_sem, w_send, w_recv, h_send, h_recv, r_send, r_recv, ok_sem, *attn,
):
    nb, nlat, nlon = sizes
    levels, rows, cols, width = tok_ref.shape
    win = WLEV * WLAT * WLON
    gw = width // GROUPS
    depth = w_ref.shape[0]
    half = depth // 2
    owid = width // OUTS
    chunks = GROUPS + OUTS
    chips = nb // 2
    nearp, diagp = edge_rows(rows)
    pad = nearp - rows
    b, lat, lon = lax.axis_index("batch"), lax.axis_index("lat"), lax.axis_index("lon")
    chip, core = b // 2, b % 2
    side = lon % 2

    def at(db=None, dlat=0, dlon=0):
        return (
            b if db is None else db,
            (lat + dlat + nlat) % nlat,
            (lon + dlon + nlon) % nlon,
        )

    partner = (chip * 2 + 1 - core, lat, lon)
    across = (b, lat, lon + 1 - 2 * side)
    far = [(((chip + k) % chips) * 2 + core, lat, lon) for k in range(1, chips)]
    beside = [at(dlon=1), at(dlon=-1)] if nlon > 2 else []
    around = [at(dlat=-1), at(dlat=1), at(dlat=-1, dlon=1), at(dlat=1, dlon=-1)]

    barrier = pltpu.get_barrier_semaphore()

    def greet(devices, to):
        for _, z, y in devices:
            pl.semaphore_signal(barrier, inc=1, device_id=(to, z, y), device_id_type=MESH)

    @pl.when(core == 1)
    def _():
        pl.semaphore_signal(barrier, inc=1, device_id=partner, device_id_type=MESH)

    for device in far:
        greet([device], device[0] // 2 * 2)
    greet([across] + beside, chip * 2)
    greet(around, chip * 2 + 1)

    def meet_near():
        @pl.when(core == 0)
        def _():
            pl.semaphore_wait(barrier, 1 + 2 * (len(far) + 1 + len(beside)))
            pl.semaphore_signal(ok_sem.at[0], inc=1, device_id=partner, device_id_type=MESH)

        @pl.when(core == 1)
        def _():
            pl.semaphore_wait(ok_sem.at[0], 1)

    def meet_around():
        @pl.when(core == 1)
        def _():
            pl.semaphore_wait(barrier, 2 * len(around))
            pl.semaphore_signal(ok_sem.at[1], inc=1, device_id=partner, device_id_type=MESH)

        @pl.when(core == 0)
        def _():
            pl.semaphore_wait(ok_sem.at[1], 1)

    def chunk(g):
        return wqkv.at[g] if g < GROUPS else wout.at[g - GROUPS]

    def own_loads(g):
        rows_here = pl.ds(pl.multiple_of(b * depth, depth), depth)
        if g >= GROUPS:
            return [pltpu.make_async_copy(
                w_ref.at[:, pl.ds(3 * width + (g - GROUPS) * owid, owid)],
                wout.at[g - GROUPS, rows_here],
                local_sem.at[2 * GROUPS + g])]
        return [
            pltpu.make_async_copy(
                w_ref.at[:, pl.ds(t * width + g * gw, gw)],
                wqkv.at[g, rows_here, pl.ds(t * gw, gw)],
                local_sem.at[3 * g + t],
            )
            for t in range(3)
        ]

    tok_load = pltpu.make_async_copy(tok_ref, own, local_sem.at[3 * GROUPS + OUTS])
    low_load = pltpu.make_async_copy(
        tok_ref.at[:, WLAT:rows], ext.at[:, 0:rows - WLAT], local_sem.at[3 * GROUPS + OUTS + 1])
    loads = [own_loads(g) for g in range(chunks)]
    for g in range(chunks):
        for c in loads[g]:
            c.start()
        if g == 0:
            tok_load.start()
    low_load.start()

    def send(src, dst, ssem, rsem, device):
        c = pltpu.make_async_remote_copy(
            src_ref=src, dst_ref=dst, send_sem=ssem, recv_sem=rsem,
            device_id=device, device_id_type=MESH,
        )
        c.start()
        return c

    steps = [(g, i * (half // CUTS), half // CUTS) for g in range(GROUPS) for i in range(CUTS)]
    steps += [(GROUPS + n, 0, half if n < OUTS - DIRECT else depth) for n in range(OUTS)]

    def whole(p):
        return steps[p][2] == depth

    def piece(p, owner, part):
        g, start, size = steps[p]
        part = 0 if whole(p) else part
        return chunk(g).at[pl.ds(pl.multiple_of(owner * depth + part * half + start, size), size)]

    sent = []
    xs, ys = {}, {}
    core_copies = {g: [] for g in range(chunks)}

    def send_w(i, ref, device):
        c = send(ref, ref, w_send.at[i], w_recv.at[i], device)
        sent.append(c)
        return c

    def slot(p, k, j):
        return chunks + (p * (chips - 1) + k - 1) * 4 + j

    def first(g):
        for c in loads[g]:
            c.wait()
        mine = chunk(g).at[pl.ds(pl.multiple_of(b * depth, depth), depth)]
        core_copies[g].append(send_w(g, mine, partner))

    def cross(p):
        for k in range(1, chips):
            xs[p, k] = send_w(slot(p, k, 0), piece(p, b, side), far[k - 1])

    def origin(k):
        return ((chip + chips - k) % chips) * 2 + core

    def relay(p):
        for k in range(1, chips):
            xs[p, k].wait_recv()
            got = piece(p, origin(k), side)
            if not whole(p):
                ys[p, k] = send_w(slot(p, k, 1), got, across)
            core_copies[steps[p][0]].append(send_w(slot(p, k, 2), got, partner))

    def finish(p):
        for k in range(1, chips if not whole(p) else 1):
            ys[p, k].wait_recv()
            core_copies[steps[p][0]].append(send_w(slot(p, k, 3), piece(p, origin(k), 1 - side), partner))

    def pump(plan):
        for kind, p in plan:
            (relay if kind == "r" else finish)(p)

    def ready(g):
        for c in core_copies[g]:
            c.wait_recv()

    shift = off_ref[0]

    def masks(ref, k):
        for i in range(rows):
            ids[i * levels:(i + 1) * levels, :] = ref[i].astype(jnp.float32)
        table = ids[...].astype(jnp.bfloat16)
        pos = lax.broadcasted_iota(jnp.int32, (levels * rows, win), 1)
        which = lax.broadcasted_iota(jnp.int32, (levels * rows, win), 0)
        pos_t = lax.broadcasted_iota(jnp.int32, (win, levels * rows), 0)
        which_t = lax.broadcasted_iota(jnp.int32, (win, levels * rows), 1)
        col = (lax.broadcasted_iota(jnp.int32, (cols, win), 0)
               == k * WLON + lax.broadcasted_iota(jnp.int32, (cols, win), 1) % WLON)
        col_t = (lax.broadcasted_iota(jnp.int32, (win, cols), 1)
                 == k * WLON + lax.broadcasted_iota(jnp.int32, (win, cols), 0) % WLON)
        wide = jnp.dot(table, col.astype(jnp.float32).astype(jnp.bfloat16), preferred_element_type=jnp.float32)
        tall = lax.dot_general(
            col_t.astype(jnp.float32).astype(jnp.bfloat16), table, (((1,), (1,)), ((), ())),
            preferred_element_type=jnp.float32)

        def row_of(p, lw):
            return (lw * WLAT + p % (WLAT * WLON) // WLON) * levels + p // (WLAT * WLON)

        for lw in range(rows // WLAT):
            r = jnp.sum(jnp.where(which == row_of(pos, lw), wide, 0.0), 0, keepdims=True)
            c = jnp.sum(jnp.where(which_t == row_of(pos_t, lw), tall, 0.0), 1, keepdims=True)
            m = (r == c).astype(jnp.float32)
            mask[lw * 2 + 1 - k] = m[:, 0:128]
            mask_rest[lw * 2 + 1 - k] = jnp.concatenate([m[:, 128:win]] * (gw // (width // HEADS)), axis=1)

    def norm(lw):
        src = own if lw == 0 else ext
        for l in range(levels):
            for ii in range(WLAT):
                x = normalise(src[l, ii + shift].astype(jnp.float32))
                base = lw * 2 * win + l * WLAT * WLON + ii * WLON
                xw[base + 1:base + WLON, :] = x[0:WLON - 1]
                xw[base + win:base + win + WLON, :] = x[WLON - 1:2 * WLON - 1]

    def norm_edges(ref, first_row, size):
        x = normalise(ref[...].astype(jnp.float32))
        for l in range(levels):
            edge_ext[l, first_row:first_row + size, :] = x[l * size:(l + 1) * size]

    def pack(lw):
        for l in range(levels):
            for ii in range(WLAT):
                base = lw * 2 * win + l * WLAT * WLON + ii * WLON
                xw[base:base + 1, :] = edge_ext[l, pl.ds(pad + lw * WLAT + ii + shift, 1), :]
        for w in range(2 * lw, 2 * lw + 2):
            xn[w * win:(w + 1) * win, :] = xw[w * win:(w + 1) * win, :].astype(jnp.bfloat16)

    def crosses(g):
        for c in loads[g]:
            c.wait()
        loads[g] = []
        for p in range(len(steps)):
            if steps[p][0] == g:
                cross(p)

    meet_near()
    crosses(0)
    first(0)
    reg_halo = send(reg_ref, reg_prev, h_send.at[1], h_recv.at[1], at(dlon=1))
    tok_load.wait()
    edge[...] = jnp.zeros_like(edge)
    for l in range(levels):
        for i in range(rows):
            row = own[l, i].astype(jnp.float32)[cols - 1:cols]
            edge[l * nearp + pad + i:l * nearp + pad + i + 1, :] = row
            if i < HALO:
                r = levels * nearp + l * diagp + i
                edge[r:r + 1, :] = row
    near[...] = edge[0:levels * nearp, :].astype(jnp.bfloat16)
    diag[...] = edge[levels * nearp:, :].astype(jnp.bfloat16)
    near_halo = send(near, near_in, h_send.at[2], h_recv.at[2], at(dlon=1))
    for g in range(1, chunks):
        crosses(g)
        first(g)
    norm(0)
    masks(reg_ref, 0)
    meet_around()
    diag_halo = send(diag, diag_in, h_send.at[3], h_recv.at[3], at(dlat=-1, dlon=1))
    lat_halo = send(tok_ref.at[:, 0:HALO], ext.at[:, rows - WLAT:rows - WLAT + HALO],
                    h_send.at[0], h_recv.at[0], at(dlat=-1))
    halos = [lat_halo, reg_halo, near_halo, diag_halo]

    hs = width // HEADS
    lane_head = lax.broadcasted_iota(jnp.int32, (win - 128, gw), 1) // hs
    for h in range(gw // hs):
        here = lax.broadcasted_iota(jnp.int32, (win, gw), 1) // hs == h
        keep[h] = jnp.where(here, hs ** -0.5, 0.0).astype(jnp.bfloat16)

    def project(g, lws):
        here = slice(lws[0] * 2 * win, (lws[-1] + 1) * 2 * win)
        for t in range(3):
            part = jnp.dot(
                xn[here, :], wqkv[g, :, t * gw:(t + 1) * gw], preferred_element_type=jnp.float32
            ).astype(jnp.bfloat16)
            for n in range(2 * len(lws)):
                qkv[g % 2, 2 * lws[0] + n, :, t * gw:(t + 1) * gw] = part[n * win:(n + 1) * win]

    def attention(g, lw, after=((), (), ())):
        pump(after[0])

        def window(w):
            q, k, v = (qkv[g % 2, lw * 2 + w, :, t * gw:(t + 1) * gw] for t in range(3))
            vt = v.T

            def softmax(scores, allowed):
                scores = jnp.where(allowed > 0.5, scores, -1e30)
                e = jnp.exp(scores - jnp.max(scores, 0, keepdims=True))
                return e.astype(jnp.bfloat16), 1.0 / jnp.sum(e, 0, keepdims=True)

            def scored(keys, queries):
                return lax.dot_general(
                    keys, queries, (((1,), (1,)), ((), ())), preferred_element_type=jnp.float32)

            for pair in range(gw // 128):
                cut = slice(pair * 128, (pair + 1) * 128)
                qp = jnp.concatenate([q[0:128, cut] * keep[h, 0:128, 0:128] for h in range(2)], axis=0)
                allowed = mask[lw * 2 + w, :, 0:128]
                e, r = softmax(scored(k[:, cut], qp), jnp.concatenate([allowed, allowed], axis=1))
                o = jnp.dot(vt[cut], e, preferred_element_type=jnp.float32) * r
                ow[w, 0:128, cut] = jnp.concatenate([o[0:hs, 0:128], o[hs:128, 128:256]], axis=0).T
            q_rest = jnp.concatenate([q[128:win] * keep[h, 128:win] for h in range(gw // hs)], axis=0)
            e, r = softmax(scored(k, q_rest), mask_rest[lw * 2 + w])
            o = (jnp.dot(vt, e, preferred_element_type=jnp.float32) * r).T
            rest = o[0:win - 128]
            for h in range(1, gw // hs):
                rest = jnp.where(lane_head == h, o[h * (win - 128):(h + 1) * (win - 128)], rest)
            ow[w, 128:win, :] = rest

        window(0)
        pump(after[1])
        window(1)
        pump(after[2])
        for l in range(levels):
            for ii in range(WLAT):
                i = lw * WLAT + ii
                r = l * WLAT * WLON + ii * WLON
                w = 0
                ret[g, l * nearp + i:l * nearp + i + 1, :] = ow[w, r:r + 1, :]
                if i >= rows - HALO:
                    d = levels * nearp + l * diagp + diagp - rows + i
                    ret[g, d:d + 1, :] = ow[w, r:r + 1, :]
                nat[l, i, 0:WLON - 1, :] = ow[w, r + 1:r + WLON, :]
                nat[l, i, WLON - 1:2 * WLON - 1, :] = ow[w + 1, r:r + WLON, :]
                attn[g][l, HALO + i] = nat[l, i].astype(jnp.bfloat16)

    def give_rows(g):
        retd[g] = ret[g, levels * nearp:, :].astype(jnp.bfloat16)
        return [
            send(attn[g].at[:, rows:rows + HALO], attn[g].at[:, 0:HALO],
                 r_send.at[3 * g], r_recv.at[3 * g], at(dlat=1)),
            send(retd.at[g], retd_in.at[g], r_send.at[3 * g + 2], r_recv.at[3 * g + 2], at(dlat=1, dlon=-1)),
        ]

    def give_edges(g):
        retn[g] = ret[g, 0:levels * nearp, :].astype(jnp.bfloat16)
        return [
            send(retn.at[g], retn_in.at[g], r_send.at[3 * g + 1], r_recv.at[3 * g + 1], at(dlon=-1)),
        ]

    nat[:, :, cols - 1:cols, :] = jnp.zeros((levels, rows, 1, gw), jnp.float32)
    ret[...] = jnp.zeros_like(ret)
    row_id = lax.broadcasted_iota(jnp.int32, (cols, gw), 0)
    backs = {}

    def gather(g):
        for c in backs[g]:
            c.wait_recv()
        n = retn_in[g].astype(jnp.float32)
        d = retd_in[g].astype(jnp.float32)
        for l in range(levels):
            ret_ext[l, 0:diagp, :] = d[l * diagp:(l + 1) * diagp]
            ret_ext[l, diagp:diagp + nearp, :] = n[l * nearp:(l + 1) * nearp]
        for l in range(levels):
            for i in range(rows):
                a = attn[g][l, HALO + i - shift].astype(jnp.float32)
                e = ret_ext[l, pl.ds(diagp + i - shift, 1), :]
                r = (l * rows + i) * cols
                ymat[r:r + cols, g * gw:(g + 1) * gw] = jnp.where(row_id == cols - 1, e, a)

    relay(0)
    near_halo.wait_recv()
    norm_edges(near_in, 0, nearp)
    pack(0)
    relay(1)
    reg_halo.wait_recv()
    masks(reg_prev, 1)
    pump(PLAN["start"])
    ready(0)
    project(0, [0])
    attention(0, 0, PLAN[0, 0])
    low_load.wait()
    diag_halo.wait_recv()
    norm_edges(diag_in, nearp, diagp)
    lat_halo.wait_recv()
    norm(1)
    pack(1)
    project(0, [1])
    attention(0, 1, PLAN[0, 1])
    backs[0] = give_rows(0) + give_edges(0)
    ready(1)
    project(1, [0, 1])
    attention(1, 1, PLAN[1, 1])
    backs[1] = give_rows(1)
    attention(1, 0, PLAN[1, 0])
    backs[1] += give_edges(1)
    ready(2)
    project(2, [0, 1])
    attention(2, 1, PLAN[2, 1])
    backs[2] = give_rows(2)
    ready(3)
    project(3, [0, 1])
    attention(3, 1, PLAN[3, 1])
    backs[3] = give_rows(3)
    attention(2, 0, PLAN[2, 0])
    backs[2] += give_edges(2)
    gather(0)
    attention(3, 0, PLAN[3, 0])
    backs[3] += give_edges(3)
    gather(1)
    gather(2)

    first_part = width - gw
    xn[:, 0:first_part] = ymat[:, 0:first_part].astype(jnp.bfloat16)
    for n in range(OUTS):
        ready(GROUPS + n)
        side_cols = slice(n * owid, (n + 1) * owid)
        p = jnp.dot(xn[:, 0:first_part], wout[n, 0:first_part], preferred_element_type=jnp.float32)
        t = own[:, :, :, side_cols].astype(jnp.float32)
        acc[:, side_cols] = t.reshape(p.shape) + p
    gather(GROUPS - 1)
    xn[:, first_part:width] = ymat[:, first_part:width].astype(jnp.bfloat16)
    for n in range(OUTS):
        side_cols = slice(n * owid, (n + 1) * owid)
        p = jnp.dot(xn[:, first_part:width], wout[n, first_part:width], preferred_element_type=jnp.float32)
        p = (acc[:, side_cols] + p).astype(jnp.bfloat16)
        out_ref[:, :, :, side_cols] = p.reshape(levels, rows, cols, owid)

    for c in sent + halos + sum(backs.values(), []):
        c.wait_send()


def edge_rows(rows):
    return -(-rows // 16) * 16, 8


def local(sizes, tokens, weights, regions, offsets):
    block = tokens[0]
    levels, rows, cols, width = block.shape
    win = WLEV * WLAT * WLON
    nwin = (rows // WLAT) * (cols // WLON)
    gw = width // GROUPS
    nearp, diagp = edge_rows(rows)
    nw = GROUPS + OUTS + 4 * (GROUPS * CUTS + OUTS) * (sizes[0] // 2 - 1)
    bf, f32 = jnp.bfloat16, jnp.float32
    dma = pltpu.SemaphoreType.DMA
    anywhere = pl.BlockSpec(memory_space=pl.ANY)
    out = pl.pallas_call(
        functools.partial(kernel, sizes),
        out_shape=pltpu.VMEM(block.shape, bf),
        in_specs=[pl.BlockSpec(memory_space=pltpu.SMEM), anywhere, anywhere, pl.BlockSpec(memory_space=pltpu.VMEM)],
        out_specs=pl.BlockSpec(memory_space=pltpu.VMEM),
        scratch_shapes=[
            pltpu.VMEM((GROUPS, width, 3 * gw), bf),
            pltpu.VMEM((OUTS, width, width // OUTS), bf),
            pltpu.VMEM((levels, rows, cols, width), bf),
            pltpu.VMEM((levels, rows - WLAT + HALO, cols, width), bf),
            pltpu.VMEM((levels * (nearp + diagp), width), f32),
            pltpu.VMEM((levels * nearp, width), bf),
            pltpu.VMEM((levels * diagp, width), bf),
            pltpu.VMEM((levels * nearp, width), bf),
            pltpu.VMEM((levels * diagp, width), bf),
            pltpu.VMEM((levels, nearp + diagp, width), f32),
            pltpu.VMEM((rows, levels, cols), jnp.int32),
            pltpu.VMEM((levels * rows, cols), f32),
            pltpu.VMEM((nwin, win, 128), f32),
            pltpu.VMEM((nwin, win, (win - 128) * HEADS // GROUPS), f32),
            pltpu.VMEM((HEADS // GROUPS, win, gw), bf),
            pltpu.VMEM((nwin * win, width), f32),
            pltpu.VMEM((nwin * win, width), bf),
            pltpu.VMEM((2, nwin, win, 3 * gw), bf),
            pltpu.VMEM((2, win, gw), f32),
            pltpu.VMEM((levels, rows, cols, gw), f32),
            pltpu.VMEM((GROUPS, levels * (nearp + diagp), gw), f32),
            pltpu.VMEM((GROUPS, levels * nearp, gw), bf),
            pltpu.VMEM((GROUPS, levels * diagp, gw), bf),
            pltpu.VMEM((GROUPS, levels * nearp, gw), bf),
            pltpu.VMEM((GROUPS, levels * diagp, gw), bf),
            pltpu.VMEM((levels, nearp + diagp, gw), f32),
            pltpu.VMEM((levels * rows * cols, width), f32),
            pltpu.VMEM((levels * rows * cols, width), f32),
            dma((3 * GROUPS + OUTS + 2,)),
            dma((nw,)),
            dma((nw,)),
            dma((4,)),
            dma((4,)),
            dma((3 * GROUPS,)),
            dma((3 * GROUPS,)),
        ]
        + [pltpu.SemaphoreType.REGULAR((2,))]
        + [pltpu.VMEM((levels, rows + HALO, cols, gw), bf)] * GROUPS,
        compiler_params=pltpu.CompilerParams(
            collective_id=0, has_side_effects=True, vmem_limit_bytes=56 * 1024 * 1024
        ),
    )(offsets, block, weights, regions.transpose(1, 0, 2))
    return out[None]


def solution(mesh):
    sizes = (mesh.shape["batch"], mesh.shape["lat"], mesh.shape["lon"])
    in_specs = (P("batch", None, "lat", "lon", None), P("batch", None), P(None, "lat", "lon"), P())
    out_specs = P("batch", None, "lat", "lon", None)
    return jax.shard_map(
        functools.partial(local, sizes), mesh=mesh, in_specs=in_specs, out_specs=out_specs, check_vma=False
    )
```

```python
import functools

import jax
import jax.numpy as jnp
from jax import lax
from jax.experimental import pallas as pl
from jax.experimental.pallas import tpu as pltpu
from jax.sharding import PartitionSpec as P

HEADS = 16
WLEV = 2
WLAT = 6
WLON = 12
GROUPS = 4
HALO = WLAT - 1
OUTS = 4
CUTS = (2, 2, 2, 2)
DIRECT = 4
MESH = pl.DeviceIdType.MESH


def plan(text):
    return tuple(tuple((e[0], int(e[1:])) for e in part.split()) for part in text.split(","))


PLAN = {
    "start": plan("r2 f0 r3 f1")[0],
    (0, 0): plan(",,r4 f2"),
    (0, 1): plan("r5 f3,,"),
    (1, 1): plan("r6 f4,,"),
    (1, 0): plan("r7 f5,,"),
    (2, 1): plan("f6,,f7 r8"),
    (3, 1): plan(",,r9"),
    (2, 0): plan(",,r10"),
    (3, 0): plan("r11,,"),
}


def normalise(x):
    average = jnp.mean(x, -1, keepdims=True)
    centred = x - average
    variance = jnp.mean(centred * centred, -1, keepdims=True)
    return centred * lax.rsqrt(variance + 1e-05)


def kernel(
    sizes,
    off_ref, tok_ref, w_ref, reg_ref, out_ref,
    wqkv, wout, own, ext, edge, near, diag, near_in, diag_in, edge_ext, reg_prev, ids, mask, mask_rest, keep, xw, xn, qkv, ow, nat,
    ret, retn, retd, retn_in, retd_in, ret_ext, ymat, acc,
    local_sem, w_send, w_recv, h_send, h_recv, r_send, r_recv, ok_sem, *attn,
):
    nb, nlat, nlon = sizes
    levels, rows, cols, width = tok_ref.shape
    win = WLEV * WLAT * WLON
    gw = width // GROUPS
    depth = w_ref.shape[0]
    half = depth // 2
    owid = width // OUTS
    chunks = GROUPS + OUTS
    chips = nb // 2
    nearp, diagp = edge_rows(rows)
    pad = nearp - rows
    b, lat, lon = lax.axis_index("batch"), lax.axis_index("lat"), lax.axis_index("lon")
    chip, core = b // 2, b % 2
    side = lon % 2

    def at(db=None, dlat=0, dlon=0):
        return (
            b if db is None else db,
            (lat + dlat + nlat) % nlat,
            (lon + dlon + nlon) % nlon,
        )

    partner = (chip * 2 + 1 - core, lat, lon)
    across = (b, lat, lon + 1 - 2 * side)
    far = [(((chip + k) % chips) * 2 + core, lat, lon) for k in range(1, chips)]
    beside = [at(dlon=1), at(dlon=-1)] if nlon > 2 else []
    around = [at(dlat=-1), at(dlat=1), at(dlat=-1, dlon=1), at(dlat=1, dlon=-1)]

    barrier = pltpu.get_barrier_semaphore()

    def greet(devices, to):
        for _, z, y in devices:
            pl.semaphore_signal(barrier, inc=1, device_id=(to, z, y), device_id_type=MESH)

    @pl.when(core == 1)
    def _():
        pl.semaphore_signal(barrier, inc=1, device_id=partner, device_id_type=MESH)

    for device in far:
        greet([device], device[0] // 2 * 2)
    greet([across] + beside, chip * 2)
    greet(around, chip * 2 + 1)

    def meet_near():
        @pl.when(core == 0)
        def _():
            pl.semaphore_wait(barrier, 1 + 2 * (len(far) + 1 + len(beside)))
            pl.semaphore_signal(ok_sem.at[0], inc=1, device_id=partner, device_id_type=MESH)

        @pl.when(core == 1)
        def _():
            pl.semaphore_wait(ok_sem.at[0], 1)

    def meet_around():
        @pl.when(core == 1)
        def _():
            pl.semaphore_wait(barrier, 2 * len(around))
            pl.semaphore_signal(ok_sem.at[1], inc=1, device_id=partner, device_id_type=MESH)

        @pl.when(core == 0)
        def _():
            pl.semaphore_wait(ok_sem.at[1], 1)

    def chunk(g):
        return wqkv.at[g] if g < GROUPS else wout.at[g - GROUPS]

    def own_loads(g):
        rows_here = pl.ds(pl.multiple_of(b * depth, depth), depth)
        if g >= GROUPS:
            return [pltpu.make_async_copy(
                w_ref.at[:, pl.ds(3 * width + (g - GROUPS) * owid, owid)],
                wout.at[g - GROUPS, rows_here],
                local_sem.at[2 * GROUPS + g])]
        return [
            pltpu.make_async_copy(
                w_ref.at[:, pl.ds(t * width + g * gw, gw)],
                wqkv.at[g, rows_here, pl.ds(t * gw, gw)],
                local_sem.at[3 * g + t],
            )
            for t in range(3)
        ]

    tok_load = pltpu.make_async_copy(tok_ref, own, local_sem.at[3 * GROUPS + OUTS])
    low_load = pltpu.make_async_copy(
        tok_ref.at[:, WLAT:rows], ext.at[:, 0:rows - WLAT], local_sem.at[3 * GROUPS + OUTS + 1])
    loads = [own_loads(g) for g in range(chunks)]
    for g in range(chunks):
        for c in loads[g]:
            c.start()
        if g == 0:
            tok_load.start()
    low_load.start()

    def send(src, dst, ssem, rsem, device):
        c = pltpu.make_async_remote_copy(
            src_ref=src, dst_ref=dst, send_sem=ssem, recv_sem=rsem,
            device_id=device, device_id_type=MESH,
        )
        c.start()
        return c

    steps = [(g, i * (half // CUTS[g]), half // CUTS[g]) for g in range(GROUPS) for i in range(CUTS[g])]
    steps += [(GROUPS + n, 0, half if n < OUTS - DIRECT else depth) for n in range(OUTS)]

    def whole(p):
        return steps[p][2] == depth

    def piece(p, owner, part):
        g, start, size = steps[p]
        part = 0 if whole(p) else part
        return chunk(g).at[pl.ds(pl.multiple_of(owner * depth + part * half + start, size), size)]

    sent = []
    xs, ys = {}, {}
    core_copies = {g: [] for g in range(chunks)}

    def send_w(i, ref, device):
        c = send(ref, ref, w_send.at[i], w_recv.at[i], device)
        sent.append(c)
        return c

    def slot(p, k, j):
        return chunks + (p * (chips - 1) + k - 1) * 4 + j

    def first(g):
        for c in loads[g]:
            c.wait()
        mine = chunk(g).at[pl.ds(pl.multiple_of(b * depth, depth), depth)]
        core_copies[g].append(send_w(g, mine, partner))

    def cross(p):
        for k in range(1, chips):
            xs[p, k] = send_w(slot(p, k, 0), piece(p, b, side), far[k - 1])

    def origin(k):
        return ((chip + chips - k) % chips) * 2 + core

    def relay(p):
        for k in range(1, chips):
            xs[p, k].wait_recv()
            got = piece(p, origin(k), side)
            if not whole(p):
                ys[p, k] = send_w(slot(p, k, 1), got, across)
            core_copies[steps[p][0]].append(send_w(slot(p, k, 2), got, partner))

    def finish(p):
        for k in range(1, chips if not whole(p) else 1):
            ys[p, k].wait_recv()
            core_copies[steps[p][0]].append(send_w(slot(p, k, 3), piece(p, origin(k), 1 - side), partner))

    def pump(plan):
        for kind, p in plan:
            (relay if kind == "r" else finish)(p)

    def ready(g):
        for c in core_copies[g]:
            c.wait_recv()

    shift = off_ref[0]

    def masks(ref, k):
        for i in range(rows):
            ids[i * levels:(i + 1) * levels, :] = ref[i].astype(jnp.float32)
        table = ids[...].astype(jnp.bfloat16)
        pos = lax.broadcasted_iota(jnp.int32, (levels * rows, win), 1)
        which = lax.broadcasted_iota(jnp.int32, (levels * rows, win), 0)
        pos_t = lax.broadcasted_iota(jnp.int32, (win, levels * rows), 0)
        which_t = lax.broadcasted_iota(jnp.int32, (win, levels * rows), 1)
        col = (lax.broadcasted_iota(jnp.int32, (cols, win), 0)
               == k * WLON + lax.broadcasted_iota(jnp.int32, (cols, win), 1) % WLON)
        col_t = (lax.broadcasted_iota(jnp.int32, (win, cols), 1)
                 == k * WLON + lax.broadcasted_iota(jnp.int32, (win, cols), 0) % WLON)
        wide = jnp.dot(table, col.astype(jnp.float32).astype(jnp.bfloat16), preferred_element_type=jnp.float32)
        tall = lax.dot_general(
            col_t.astype(jnp.float32).astype(jnp.bfloat16), table, (((1,), (1,)), ((), ())),
            preferred_element_type=jnp.float32)

        def row_of(p, lw):
            return (lw * WLAT + p % (WLAT * WLON) // WLON) * levels + p // (WLAT * WLON)

        for lw in range(rows // WLAT):
            r = jnp.sum(jnp.where(which == row_of(pos, lw), wide, 0.0), 0, keepdims=True)
            c = jnp.sum(jnp.where(which_t == row_of(pos_t, lw), tall, 0.0), 1, keepdims=True)
            m = (r == c).astype(jnp.float32)
            mask[lw * 2 + 1 - k] = m[:, 0:128]
            mask_rest[lw * 2 + 1 - k] = jnp.concatenate([m[:, 128:win]] * (gw // (width // HEADS)), axis=1)

    def norm(lw):
        src = own if lw == 0 else ext
        for l in range(levels):
            for ii in range(WLAT):
                x = normalise(src[l, ii + shift].astype(jnp.float32))
                base = lw * 2 * win + l * WLAT * WLON + ii * WLON
                xw[base + 1:base + WLON, :] = x[0:WLON - 1]
                xw[base + win:base + win + WLON, :] = x[WLON - 1:2 * WLON - 1]

    def norm_edges(ref, first_row, size):
        x = normalise(ref[...].astype(jnp.float32))
        for l in range(levels):
            edge_ext[l, first_row:first_row + size, :] = x[l * size:(l + 1) * size]

    def pack(lw):
        for l in range(levels):
            for ii in range(WLAT):
                base = lw * 2 * win + l * WLAT * WLON + ii * WLON
                xw[base:base + 1, :] = edge_ext[l, pl.ds(pad + lw * WLAT + ii + shift, 1), :]
        for w in range(2 * lw, 2 * lw + 2):
            xn[w * win:(w + 1) * win, :] = xw[w * win:(w + 1) * win, :].astype(jnp.bfloat16)

    def crosses(g):
        for c in loads[g]:
            c.wait()
        loads[g] = []
        for p in range(len(steps)):
            if steps[p][0] == g:
                cross(p)

    meet_near()
    crosses(0)
    first(0)
    for g in range(1, chunks):
        crosses(g)
    meet_around()
    lat_halo = send(tok_ref.at[:, 0:HALO], ext.at[:, rows - WLAT:rows - WLAT + HALO],
                    h_send.at[0], h_recv.at[0], at(dlat=-1))
    reg_halo = send(reg_ref, reg_prev, h_send.at[1], h_recv.at[1], at(dlon=1))
    tok_load.wait()
    edge[...] = jnp.zeros_like(edge)
    for l in range(levels):
        for i in range(rows):
            row = own[l, i].astype(jnp.float32)[cols - 1:cols]
            edge[l * nearp + pad + i:l * nearp + pad + i + 1, :] = row
            if i < HALO:
                r = levels * nearp + l * diagp + i
                edge[r:r + 1, :] = row
    near[...] = edge[0:levels * nearp, :].astype(jnp.bfloat16)
    diag[...] = edge[levels * nearp:, :].astype(jnp.bfloat16)
    near_halo = send(near, near_in, h_send.at[2], h_recv.at[2], at(dlon=1))
    diag_halo = send(diag, diag_in, h_send.at[3], h_recv.at[3], at(dlat=-1, dlon=1))
    for g in range(1, chunks):
        first(g)
    norm(0)
    masks(reg_ref, 0)
    halos = [lat_halo, reg_halo, near_halo, diag_halo]

    hs = width // HEADS
    lane_head = lax.broadcasted_iota(jnp.int32, (win - 128, gw), 1) // hs
    for h in range(gw // hs):
        here = lax.broadcasted_iota(jnp.int32, (win, gw), 1) // hs == h
        keep[h] = jnp.where(here, hs ** -0.5, 0.0).astype(jnp.bfloat16)

    def project(g, lws):
        here = slice(lws[0] * 2 * win, (lws[-1] + 1) * 2 * win)
        for t in range(3):
            part = jnp.dot(
                xn[here, :], wqkv[g, :, t * gw:(t + 1) * gw], preferred_element_type=jnp.float32
            ).astype(jnp.bfloat16)
            for n in range(2 * len(lws)):
                qkv[g % 2, 2 * lws[0] + n, :, t * gw:(t + 1) * gw] = part[n * win:(n + 1) * win]

    def attention(g, lw, after=((), (), ())):
        pump(after[0])

        def window(w):
            q, k, v = (qkv[g % 2, lw * 2 + w, :, t * gw:(t + 1) * gw] for t in range(3))
            vt = v.T

            def softmax(scores, allowed):
                scores = jnp.where(allowed > 0.5, scores, -1e30)
                e = jnp.exp(scores - jnp.max(scores, 0, keepdims=True))
                return e.astype(jnp.bfloat16), 1.0 / jnp.sum(e, 0, keepdims=True)

            def scored(keys, queries):
                return lax.dot_general(
                    keys, queries, (((1,), (1,)), ((), ())), preferred_element_type=jnp.float32)

            for pair in range(gw // 128):
                cut = slice(pair * 128, (pair + 1) * 128)
                qp = jnp.concatenate([q[0:128, cut] * keep[h, 0:128, 0:128] for h in range(2)], axis=0)
                allowed = mask[lw * 2 + w, :, 0:128]
                e, r = softmax(scored(k[:, cut], qp), jnp.concatenate([allowed, allowed], axis=1))
                o = jnp.dot(vt[cut], e, preferred_element_type=jnp.float32) * r
                ow[w, 0:128, cut] = jnp.concatenate([o[0:hs, 0:128], o[hs:128, 128:256]], axis=0).T
            q_rest = jnp.concatenate([q[128:win] * keep[h, 128:win] for h in range(gw // hs)], axis=0)
            e, r = softmax(scored(k, q_rest), mask_rest[lw * 2 + w])
            o = (jnp.dot(vt, e, preferred_element_type=jnp.float32) * r).T
            rest = o[0:win - 128]
            for h in range(1, gw // hs):
                rest = jnp.where(lane_head == h, o[h * (win - 128):(h + 1) * (win - 128)], rest)
            ow[w, 128:win, :] = rest

        window(0)
        pump(after[1])
        window(1)
        pump(after[2])
        for l in range(levels):
            for ii in range(WLAT):
                i = lw * WLAT + ii
                r = l * WLAT * WLON + ii * WLON
                w = 0
                ret[g, l * nearp + i:l * nearp + i + 1, :] = ow[w, r:r + 1, :]
                if i >= rows - HALO:
                    d = levels * nearp + l * diagp + diagp - rows + i
                    ret[g, d:d + 1, :] = ow[w, r:r + 1, :]
                nat[l, i, 0:WLON - 1, :] = ow[w, r + 1:r + WLON, :]
                nat[l, i, WLON - 1:2 * WLON - 1, :] = ow[w + 1, r:r + WLON, :]
                attn[g][l, HALO + i] = nat[l, i].astype(jnp.bfloat16)

    def give_rows(g):
        retd[g] = ret[g, levels * nearp:, :].astype(jnp.bfloat16)
        return [
            send(attn[g].at[:, rows:rows + HALO], attn[g].at[:, 0:HALO],
                 r_send.at[3 * g], r_recv.at[3 * g], at(dlat=1)),
            send(retd.at[g], retd_in.at[g], r_send.at[3 * g + 2], r_recv.at[3 * g + 2], at(dlat=1, dlon=-1)),
        ]

    def give_edges(g):
        retn[g] = ret[g, 0:levels * nearp, :].astype(jnp.bfloat16)
        return [
            send(retn.at[g], retn_in.at[g], r_send.at[3 * g + 1], r_recv.at[3 * g + 1], at(dlon=-1)),
        ]

    nat[:, :, cols - 1:cols, :] = jnp.zeros((levels, rows, 1, gw), jnp.float32)
    ret[...] = jnp.zeros_like(ret)
    row_id = lax.broadcasted_iota(jnp.int32, (cols, gw), 0)
    backs = {}

    def gather(g):
        for c in backs[g]:
            c.wait_recv()
        n = retn_in[g].astype(jnp.float32)
        d = retd_in[g].astype(jnp.float32)
        for l in range(levels):
            ret_ext[l, 0:diagp, :] = d[l * diagp:(l + 1) * diagp]
            ret_ext[l, diagp:diagp + nearp, :] = n[l * nearp:(l + 1) * nearp]
        for l in range(levels):
            for i in range(rows):
                a = attn[g][l, HALO + i - shift].astype(jnp.float32)
                e = ret_ext[l, pl.ds(diagp + i - shift, 1), :]
                r = (l * rows + i) * cols
                ymat[r:r + cols, g * gw:(g + 1) * gw] = jnp.where(row_id == cols - 1, e, a)

    relay(0)
    near_halo.wait_recv()
    norm_edges(near_in, 0, nearp)
    pack(0)
    relay(1)
    pump(PLAN["start"])
    reg_halo.wait_recv()
    masks(reg_prev, 1)
    ready(0)
    project(0, [0])
    attention(0, 0, PLAN[0, 0])
    low_load.wait()
    diag_halo.wait_recv()
    norm_edges(diag_in, nearp, diagp)
    lat_halo.wait_recv()
    norm(1)
    pack(1)
    project(0, [1])
    attention(0, 1, PLAN[0, 1])
    backs[0] = give_rows(0) + give_edges(0)
    ready(1)
    project(1, [0, 1])
    attention(1, 1, PLAN[1, 1])
    backs[1] = give_rows(1)
    attention(1, 0, PLAN[1, 0])
    backs[1] += give_edges(1)
    ready(2)
    project(2, [0, 1])
    attention(2, 1, PLAN[2, 1])
    backs[2] = give_rows(2)
    gather(0)
    ready(3)
    project(3, [0, 1])
    attention(3, 1, PLAN[3, 1])
    backs[3] = give_rows(3)
    attention(2, 0, PLAN[2, 0])
    backs[2] += give_edges(2)
    attention(3, 0, PLAN[3, 0])
    backs[3] += give_edges(3)
    gather(1)
    gather(2)

    first_part = width - gw
    xn[:, 0:first_part] = ymat[:, 0:first_part].astype(jnp.bfloat16)
    for n in range(OUTS):
        ready(GROUPS + n)
        side_cols = slice(n * owid, (n + 1) * owid)
        p = jnp.dot(xn[:, 0:first_part], wout[n, 0:first_part], preferred_element_type=jnp.float32)
        t = own[:, :, :, side_cols].astype(jnp.float32)
        acc[:, side_cols] = t.reshape(p.shape) + p
    gather(GROUPS - 1)
    xn[:, first_part:width] = ymat[:, first_part:width].astype(jnp.bfloat16)
    for n in range(OUTS):
        side_cols = slice(n * owid, (n + 1) * owid)
        p = jnp.dot(xn[:, first_part:width], wout[n, first_part:width], preferred_element_type=jnp.float32)
        p = (acc[:, side_cols] + p).astype(jnp.bfloat16)
        out_ref[:, :, :, side_cols] = p.reshape(levels, rows, cols, owid)

    for c in sent + halos + sum(backs.values(), []):
        c.wait_send()


def edge_rows(rows):
    return -(-rows // 16) * 16, 8


def local(sizes, tokens, weights, regions, offsets):
    block = tokens[0]
    levels, rows, cols, width = block.shape
    win = WLEV * WLAT * WLON
    nwin = (rows // WLAT) * (cols // WLON)
    gw = width // GROUPS
    nearp, diagp = edge_rows(rows)
    nw = GROUPS + OUTS + 4 * (sum(CUTS) + OUTS) * (sizes[0] // 2 - 1)
    bf, f32 = jnp.bfloat16, jnp.float32
    dma = pltpu.SemaphoreType.DMA
    anywhere = pl.BlockSpec(memory_space=pl.ANY)
    out = pl.pallas_call(
        functools.partial(kernel, sizes),
        out_shape=pltpu.VMEM(block.shape, bf),
        in_specs=[pl.BlockSpec(memory_space=pltpu.SMEM), anywhere, anywhere, pl.BlockSpec(memory_space=pltpu.VMEM)],
        out_specs=pl.BlockSpec(memory_space=pltpu.VMEM),
        scratch_shapes=[
            pltpu.VMEM((GROUPS, width, 3 * gw), bf),
            pltpu.VMEM((OUTS, width, width // OUTS), bf),
            pltpu.VMEM((levels, rows, cols, width), bf),
            pltpu.VMEM((levels, rows - WLAT + HALO, cols, width), bf),
            pltpu.VMEM((levels * (nearp + diagp), width), f32),
            pltpu.VMEM((levels * nearp, width), bf),
            pltpu.VMEM((levels * diagp, width), bf),
            pltpu.VMEM((levels * nearp, width), bf),
            pltpu.VMEM((levels * diagp, width), bf),
            pltpu.VMEM((levels, nearp + diagp, width), f32),
            pltpu.VMEM((rows, levels, cols), jnp.int32),
            pltpu.VMEM((levels * rows, cols), f32),
            pltpu.VMEM((nwin, win, 128), f32),
            pltpu.VMEM((nwin, win, (win - 128) * HEADS // GROUPS), f32),
            pltpu.VMEM((HEADS // GROUPS, win, gw), bf),
            pltpu.VMEM((nwin * win, width), f32),
            pltpu.VMEM((nwin * win, width), bf),
            pltpu.VMEM((2, nwin, win, 3 * gw), bf),
            pltpu.VMEM((2, win, gw), f32),
            pltpu.VMEM((levels, rows, cols, gw), f32),
            pltpu.VMEM((GROUPS, levels * (nearp + diagp), gw), f32),
            pltpu.VMEM((GROUPS, levels * nearp, gw), bf),
            pltpu.VMEM((GROUPS, levels * diagp, gw), bf),
            pltpu.VMEM((GROUPS, levels * nearp, gw), bf),
            pltpu.VMEM((GROUPS, levels * diagp, gw), bf),
            pltpu.VMEM((levels, nearp + diagp, gw), f32),
            pltpu.VMEM((levels * rows * cols, width), f32),
            pltpu.VMEM((levels * rows * cols, width), f32),
            dma((3 * GROUPS + OUTS + 2,)),
            dma((nw,)),
            dma((nw,)),
            dma((4,)),
            dma((4,)),
            dma((3 * GROUPS,)),
            dma((3 * GROUPS,)),
        ]
        + [pltpu.SemaphoreType.REGULAR((2,))]
        + [pltpu.VMEM((levels, rows + HALO, cols, gw), bf)] * GROUPS,
        compiler_params=pltpu.CompilerParams(
            collective_id=0, has_side_effects=True, vmem_limit_bytes=56 * 1024 * 1024
        ),
    )(offsets, block, weights, regions.transpose(1, 0, 2))
    return out[None]


def solution(mesh):
    sizes = (mesh.shape["batch"], mesh.shape["lat"], mesh.shape["lon"])
    in_specs = (P("batch", None, "lat", "lon", None), P("batch", None), P(None, "lat", "lon"), P())
    out_specs = P("batch", None, "lat", "lon", None)
    return jax.shard_map(
        functools.partial(local, sizes), mesh=mesh, in_specs=in_specs, out_specs=out_specs, check_vma=False
    )
```
